32 devices in a mesh: groups: 2 (over x), pb: 16 (over z, y, core).
Axes of the slice: x: 2, y: 2, z: 4, core: 2. Of those that a mesh axis runs over, the one named last changes fastest.
Arguments:
- frames: float32 [64, 512, 2048], P(('groups', 'pb')), parts along dimension 0, as said below
- valid_mask: int32 [64], P(('groups', 'pb')), parts along dimension 0, may hold values from 0 to 1, as said below
Outputs:
- correlations: float32 [128, 512, 512], P('groups', 'pb'), parts along dimension 0
The draws below stay inside these ranges and needn't reach their ends.
There are 2 independent parts, one for each index of `groups`. The reference program is written for one: setup_inputs(seed, part) draws one part's arguments, and reference() takes and returns one part's arrays. A program takes and returns all parts, laid end to end along the dimension named above; each array names one. Nothing has to cross between parts.
Inputs may be any that keep to these rules, and one draw needn't show every extreme that they name: `valid_mask`: the window holds at least one valid shot; the aligned blocks of 2 shots (the shots of one index of pb) may differ in their rate of valid shots. `frames`: frames share an anisotropic pattern across shots beside independent fluctuations.
All inputs are finite; a program needn't handle non-finite values.
Results may differ from the reference program's by a relative error of at most 0.02.
Values may be sent and summed in bfloat16 or wider, within the bound.
No kernel may reach another device: no remote copies, remote signals or barrier semaphores. Data moves between devices by JAX's collectives and lax.ppermute only.
A program may use at most 128 MiB of HBM per device.

```python
import math
import jax
import jax.numpy as jnp
from jax import lax

CYCLES = 512
ANGLES = 2048
HARMONICS = 64
SHOT_DEV = 2
SHOTS = 32


def draw_frames(key, part):
    key_common = jax.random.fold_in(key, 11)
    key_shot = jax.random.fold_in(key, 12)
    common = jax.random.normal(key_common, (CYCLES, ANGLES), jnp.float32)
    noise = jax.random.normal(key_shot, (SHOTS, CYCLES, ANGLES), jnp.float32)
    return common[None, :, :] + noise


def draw_valid_mask(key, part):
    shards = SHOTS // SHOT_DEV
    key_rate = jax.random.fold_in(key, 21)
    key_roll = jax.random.fold_in(key, 22)
    key_keep = jax.random.fold_in(key, 23)
    rate_level = jax.random.randint(key_rate, (shards, 1), 1, 5)
    roll_value = jax.random.randint(key_roll, (shards, SHOT_DEV), 0, 5)
    chosen = (roll_value < rate_level).astype(jnp.int32).reshape(SHOTS)
    keep_index = jax.random.randint(key_keep, (), 0, SHOTS)
    position = jnp.arange(SHOTS, dtype=jnp.int32)
    forced = (position == keep_index).astype(jnp.int32)
    return jnp.maximum(chosen, forced)


def setup_inputs(seed: int = 0, part: int = 0) -> dict:
    key_of = jax.random.split(jax.random.key(seed), 3)
    own_keys = jax.random.split(jax.random.fold_in(key_of[2], part), 3)
    frames = draw_frames(jax.random.fold_in(jax.random.fold_in(key_of[2], part), 71), part)
    valid_mask = draw_valid_mask(jax.random.fold_in(jax.random.fold_in(key_of[2], part), 71), part)
    return {"frames": frames, "valid_mask": valid_mask}


def angle_table(angles, harmonics):
    harmonic_order = 2 * (jnp.arange(harmonics, dtype=jnp.int32) + 1)
    angle_index = jnp.arange(angles, dtype=jnp.int32)
    wrapped = angle_index[:, None] * harmonic_order[None, :] % angles
    phase_angle = wrapped.astype(jnp.float32) * (2.0 * math.pi / angles)
    scale_factor = 1.0 / math.sqrt(angles)
    return jnp.concatenate([jnp.cos(phase_angle), -jnp.sin(phase_angle)], axis=1) * scale_factor

def reference(frames, valid_mask):
    phase_table = angle_table(ANGLES, HARMONICS)
    weights = valid_mask.astype(jnp.float32)

    def transform_shot(pair):
        frame_one, weight_one = pair
        projected = jnp.dot(frame_one, phase_table, precision=lax.Precision.HIGHEST)
        return (weight_one * projected).astype(jnp.bfloat16)
    spectra = lax.map(transform_shot, (frames, weights))
    valid_total = jnp.sum(weights)
    spectra_wide = spectra.astype(jnp.float32)
    mean_cycles = lax.optimization_barrier(jnp.sum(spectra_wide, axis=0)) / valid_total
    split_spectra = spectra_wide.reshape(SHOTS, CYCLES, 2, HARMONICS)
    panel = jnp.einsum('sqcn,spcn->nqp', split_spectra, split_spectra, precision=lax.Precision.HIGHEST)
    split_mean = mean_cycles.reshape(CYCLES, 2, HARMONICS)
    outer_mean = jnp.einsum('qcn,pcn->nqp', split_mean, split_mean, precision=lax.Precision.HIGHEST)
    return panel / valid_total - outer_mean
```

```python
import functools
import math

import jax
import jax.numpy as jnp
import numpy as np
from jax import lax
from jax.experimental import pallas as pl
from jax.experimental.pallas import tpu as pltpu
from jax.sharding import PartitionSpec as P

HARMONICS = 64
LANES = 128
GROUP = 4
ROWS = 4 * GROUP
CHUNKS = 2


def half_table(angles):
    order = 2 * (np.arange(HARMONICS) + 1)
    wrapped = np.arange(angles // 2)[:, None] * order[None, :] % angles
    phase = wrapped * (2.0 * math.pi / angles)
    table = np.stack([np.cos(phase), -np.sin(phase)], axis=-1).reshape(angles // 2, 2 * HARMONICS)
    table = (2.0 / math.sqrt(angles)) * table
    high = table.astype(jnp.bfloat16)
    low = (table - high.astype(np.float64)).astype(jnp.bfloat16)
    return np.concatenate([high, low], axis=1)


def spectra_kernel(mask_ref, frames_ref, table_ref, *refs):
    out_refs = refs[:CHUNKS]
    buf, table, sems = refs[CHUNKS:]
    shots, cycles, angles = frames_ref.shape
    blocks = cycles // LANES
    half = angles // 2
    groups = HARMONICS // GROUP // CHUNKS
    copies = [pltpu.make_async_copy(table_ref, table, sems.at[shots * blocks])]
    for q in range(blocks):
        for s in range(shots):
            copies.append(
                pltpu.make_async_copy(
                    frames_ref.at[s, pl.ds(q * LANES, LANES), :], buf.at[q * shots + s], sems.at[q * shots + s]
                )
            )
    for copy in copies:
        copy.start()
    weights = [mask_ref[s].astype(jnp.float32) for s in range(shots)]
    row = lax.broadcasted_iota(jnp.int32, (ROWS, LANES), 0)
    tile = jnp.where(row < ROWS // 2, weights[0], weights[1]).astype(jnp.bfloat16)
    out_refs[0][pl.ds(groups * blocks * ROWS, ROWS), :] = tile
    copies[0].wait()
    for q in range(blocks):
        turned = []
        for s in range(shots):
            copies[1 + q * shots + s].wait()
            scale = 0.5 * weights[s]
            x = buf[q * shots + s]
            folded = x[:, :half] * scale + x[:, half:] * scale
            high = folded.astype(jnp.bfloat16)
            low = (folded - high.astype(jnp.float32)).astype(jnp.bfloat16)
            pair = jnp.dot(high, table[...], preferred_element_type=jnp.float32)
            pair += jnp.dot(low, table[...], preferred_element_type=jnp.float32)
            turned.append((pair[:, :LANES] + pair[:, LANES:]).T)
        for g in range(HARMONICS // GROUP):
            part = slice(g * 2 * GROUP, (g + 1) * 2 * GROUP)
            block = jnp.concatenate([turned[0][part], turned[1][part]], axis=0).astype(jnp.bfloat16)
            out_refs[g // groups][pl.ds((g % groups * blocks + q) * ROWS, ROWS), :] = block


def spectra_call(frames, valid_mask):
    shots, cycles, angles = frames.shape
    blocks = cycles // LANES
    groups = HARMONICS // GROUP // CHUNKS
    rows = [groups * blocks * ROWS + (ROWS if c == 0 else 0) for c in range(CHUNKS)]
    table = jnp.asarray(half_table(angles))
    return pl.pallas_call(
        spectra_kernel,
        out_shape=[jax.ShapeDtypeStruct((r, LANES), jnp.bfloat16) for r in rows],
        in_specs=[
            pl.BlockSpec(memory_space=pltpu.SMEM),
            pl.BlockSpec(memory_space=pl.ANY),
            pl.BlockSpec(memory_space=pl.ANY),
        ],
        out_specs=[pl.BlockSpec(memory_space=pltpu.VMEM)] * CHUNKS,
        scratch_shapes=[
            pltpu.VMEM((shots * blocks, LANES, angles), jnp.float32),
            pltpu.VMEM(table.shape, jnp.bfloat16),
            pltpu.SemaphoreType.DMA((shots * blocks + 1,)),
        ],
        compiler_params=pltpu.CompilerParams(vmem_limit_bytes=20 << 20),
        cost_estimate=pl.CostEstimate(
            flops=8 * shots * cycles * angles * LANES, bytes_accessed=frames.size * 4, transcendentals=0
        ),
        name="spectra",
    )(valid_mask, frames, table)


def correlate_kernel(shared, start_ref, *refs):
    n = shared["n"]
    pieces, firsts = refs[:n], refs[n : 2 * n]
    out_ref, centred, pick, weight, inverse = refs[-5:]
    width = out_ref.shape[1]
    cycles = out_ref.shape[2]
    blocks = cycles // LANES
    tail = shared["tail"]
    start = start_ref[0]
    step = pl.program_id(0)

    @pl.when(step == 0)
    def _():
        lane = lax.broadcasted_iota(jnp.int32, (GROUP * width, LANES), 1)
        line = lax.broadcasted_iota(jnp.int32, (GROUP * width, LANES), 0)
        pick[...] = jnp.where(lane == start % LANES + line % width, 1.0, 0.0).astype(jnp.bfloat16)
        total = jnp.zeros((ROWS // 2, LANES), jnp.float32)
        for d in range(n):
            tile = firsts[d][pl.ds(tail, ROWS), :].astype(jnp.float32)
            weight[d] = tile
            total += tile[: ROWS // 2] + tile[ROWS // 2 :]
        inverse[...] = 1.0 / total

    scale = inverse[...]
    for q in range(blocks):
        where = pl.ds(pl.multiple_of((step * blocks + q) * ROWS, ROWS), ROWS)
        total = jnp.zeros((ROWS, LANES), jnp.float32)
        for d in range(n):
            total += pieces[d][where, :].astype(jnp.float32)
        mean = (total[: ROWS // 2] + total[ROWS // 2 :]) * scale
        mean = jnp.concatenate([mean, mean], axis=0)
        for d in range(n):
            tile = (pieces[d][where, :].astype(jnp.float32) - mean) * weight[d]
            centred[pl.ds(d * ROWS, ROWS), pl.ds(q * LANES, LANES)] = tile.astype(jnp.bfloat16)
    own = centred[:, pl.ds(pl.multiple_of(start // LANES * LANES, LANES), LANES)]
    left = lax.dot_general(pick[...], own, (((1,), (1,)), ((), ())), preferred_element_type=jnp.float32)
    line = lax.broadcasted_iota(jnp.int32, left.shape, 0) // width
    lane = lax.broadcasted_iota(jnp.int32, left.shape, 1) % (2 * GROUP) // 2
    left = jnp.where(line == lane, left, 0.0).astype(jnp.bfloat16)
    product = jnp.dot(left, centred[...], preferred_element_type=jnp.float32)
    product = product * scale[:1, :1]
    out_ref[...] = product.reshape(GROUP, width, cycles)


def correlate_call(start, pieces, firsts, before, chunk, cycles, tail):
    n = len(pieces)
    width = cycles // n
    groups = HARMONICS // GROUP // CHUNKS
    operands = [start, *pieces, *firsts]
    specs = [pl.BlockSpec(memory_space=pltpu.SMEM)] + [pl.BlockSpec(memory_space=pltpu.VMEM)] * (2 * n)
    aliases = {}
    if before is not None:
        aliases = {len(operands): 0}
        operands.append(before)
        specs.append(pl.BlockSpec(memory_space=pl.ANY))
    return pl.pallas_call(
        functools.partial(correlate_kernel, {"n": n, "tail": tail}),
        out_shape=jax.ShapeDtypeStruct((HARMONICS, width, cycles), jnp.float32),
        grid=(groups,),
        in_specs=specs,
        out_specs=pl.BlockSpec((GROUP, width, cycles), lambda g: (g + chunk * groups, 0, 0)),
        scratch_shapes=[
            pltpu.VMEM((n * ROWS, cycles), jnp.bfloat16),
            pltpu.VMEM((GROUP * width, LANES), jnp.bfloat16),
            pltpu.VMEM((n, ROWS, LANES), jnp.float32),
            pltpu.VMEM((ROWS // 2, LANES), jnp.float32),
        ],
        input_output_aliases=aliases,
        compiler_params=pltpu.CompilerParams(vmem_limit_bytes=24 << 20),
        cost_estimate=pl.CostEstimate(
            flops=2 * HARMONICS // CHUNKS * width * cycles * n * ROWS,
            bytes_accessed=HARMONICS // CHUNKS * width * cycles * 4,
            transcendentals=0,
        ),
        name="correlate",
    )(*operands)


def gather(piece, n):
    def swap(x, bits):
        return lax.ppermute(x, "pb", [(i, i ^ bits) for i in range(n)])

    held = [piece]
    if n == 16:
        near = swap(piece, 4)
        far = swap(piece, 12)
        held += [near, far, swap(far, 4)]
        held += [swap(x, 2) for x in held]
        held += [swap(x, 1) for x in held]
        return held
    bit = n // 2
    while bit:
        held += [swap(x, bit) for x in held]
        bit //= 2
    return held


def body(frames, valid_mask):
    shots, cycles, angles = frames.shape
    n = lax.axis_size("pb")
    parts = spectra_call(frames, valid_mask)
    start = (lax.axis_index("pb") * (cycles // n)).astype(jnp.int32).reshape(1)
    held = [gather(part, n) for part in parts]
    tail = parts[0].shape[0] - ROWS
    out = None
    for chunk in range(CHUNKS):
        out = correlate_call(start, held[chunk], held[0], out, chunk, cycles, tail)
    return out


def solution(mesh):
    placed = (P(("groups", "pb"), None, None), P(("groups", "pb")))
    return jax.shard_map(
        body, mesh=mesh, in_specs=placed, out_specs=P("groups", "pb", None), check_vma=False
    )
```

```python
import functools
import math

import jax
import jax.numpy as jnp
import numpy as np
from jax import lax
from jax.experimental import pallas as pl
from jax.experimental.pallas import tpu as pltpu
from jax.sharding import PartitionSpec as P

HARMONICS = 64
LANES = 128
GROUP = 4
ROWS = 4 * GROUP
CHUNKS = 2
DEPTH = 256


def half_table(angles):
    order = 2 * (np.arange(HARMONICS) + 1)
    wrapped = np.arange(angles // 2)[:, None] * order[None, :] % angles
    phase = wrapped * (2.0 * math.pi / angles)
    table = np.stack([np.cos(phase), -np.sin(phase)], axis=-1).reshape(angles // 2, 2 * HARMONICS)
    table = (2.0 / math.sqrt(angles)) * table
    high = table.astype(jnp.bfloat16)
    low = (table - high.astype(np.float64)).astype(jnp.bfloat16)
    return np.concatenate([high, low], axis=1)


def spectra_kernel(mask_ref, frames_ref, table_ref, *refs):
    out_refs = refs[:CHUNKS]
    buf, table, halves, sems = refs[CHUNKS:]
    shots, cycles, angles = frames_ref.shape
    blocks = cycles // LANES
    half = angles // 2
    groups = HARMONICS // GROUP // CHUNKS
    copies = [pltpu.make_async_copy(table_ref, table, sems.at[shots * blocks])]
    for q in range(blocks):
        for s in range(shots):
            copies.append(
                pltpu.make_async_copy(
                    frames_ref.at[s, pl.ds(q * LANES, LANES), :], buf.at[q * shots + s], sems.at[q * shots + s]
                )
            )
    for copy in copies:
        copy.start()
    weights = [mask_ref[s].astype(jnp.float32) for s in range(shots)]
    row = lax.broadcasted_iota(jnp.int32, (ROWS, LANES), 0)
    tile = jnp.where(row < ROWS // 2, weights[0], weights[1]).astype(jnp.bfloat16)
    out_refs[0][pl.ds(groups * blocks * ROWS, ROWS), :] = tile
    copies[0].wait()

    def split(q, s, k):
        scale = 0.5 * weights[s]
        x = buf.at[q * shots + s]
        folded = x[:, pl.ds(k, DEPTH)] * scale + x[:, pl.ds(half + k, DEPTH)] * scale
        high = folded.astype(jnp.bfloat16)
        halves[q % 2, s, pl.ds(0, LANES), pl.ds(k, DEPTH)] = high
        halves[q % 2, s, pl.ds(LANES, LANES), pl.ds(k, DEPTH)] = (folded - high.astype(jnp.float32)).astype(jnp.bfloat16)

    for s in range(shots):
        copies[1 + s].wait()
        for k in range(0, half, DEPTH):
            split(0, s, k)
    for q in range(blocks):
        if q + 1 < blocks:
            for s in range(shots):
                copies[1 + (q + 1) * shots + s].wait()
        pairs = [jnp.zeros((2 * LANES, 2 * LANES), jnp.float32)] * shots
        for k in range(0, half, DEPTH):
            for s in range(shots):
                pairs[s] += jnp.dot(
                    halves[q % 2, s, :, pl.ds(k, DEPTH)], table[pl.ds(k, DEPTH), :], preferred_element_type=jnp.float32
                )
                if q + 1 < blocks:
                    split(q + 1, s, k)
        turned = []
        for pair in pairs:
            pair = pair[:LANES] + pair[LANES:]
            turned.append((pair[:, :LANES] + pair[:, LANES:]).T)
        for g in range(HARMONICS // GROUP):
            part = slice(g * 2 * GROUP, (g + 1) * 2 * GROUP)
            block = jnp.concatenate([turned[0][part], turned[1][part]], axis=0).astype(jnp.bfloat16)
            out_refs[g // groups][pl.ds((g % groups * blocks + q) * ROWS, ROWS), :] = block


def spectra_call(frames, valid_mask):
    shots, cycles, angles = frames.shape
    blocks = cycles // LANES
    groups = HARMONICS // GROUP // CHUNKS
    rows = [groups * blocks * ROWS + (ROWS if c == 0 else 0) for c in range(CHUNKS)]
    table = jnp.asarray(half_table(angles))
    return pl.pallas_call(
        spectra_kernel,
        out_shape=[jax.ShapeDtypeStruct((r, LANES), jnp.bfloat16) for r in rows],
        in_specs=[
            pl.BlockSpec(memory_space=pltpu.SMEM),
            pl.BlockSpec(memory_space=pltpu.HBM),
            pl.BlockSpec(memory_space=pltpu.HBM),
        ],
        out_specs=[pl.BlockSpec(memory_space=pltpu.VMEM)] * CHUNKS,
        scratch_shapes=[
            pltpu.VMEM((shots * blocks, LANES, angles), jnp.float32),
            pltpu.VMEM(table.shape, jnp.bfloat16),
            pltpu.VMEM((2, shots, 2 * LANES, angles // 2), jnp.bfloat16),
            pltpu.SemaphoreType.DMA((shots * blocks + 1,)),
        ],
        compiler_params=pltpu.CompilerParams(vmem_limit_bytes=60 << 20),
        cost_estimate=pl.CostEstimate(
            flops=8 * shots * cycles * angles * LANES, bytes_accessed=frames.size * 4, transcendentals=0
        ),
        name="spectra",
    )(valid_mask, frames, table)


def correlate_kernel(tail, start_ref, *refs):
    out_ref, left, inverse = refs[-3:]
    n = left.shape[2] // ROWS
    pieces, firsts = refs[:n], refs[n : 2 * n]
    per_step = out_ref.shape[0] // GROUP
    width, cycles = out_ref.shape[1:]
    blocks = cycles // LANES
    wide = GROUP * width
    step = pl.program_id(0)

    def tiles(group, q):
        where = pl.ds(pl.multiple_of((group * blocks + q) * ROWS, ROWS), ROWS)
        return jnp.concatenate([piece[where, :] for piece in pieces], axis=0)

    @pl.when(step == 0)
    def _():
        total = jnp.zeros((ROWS // 2, LANES), jnp.float32)
        for first in firsts:
            tile = first[pl.ds(tail, ROWS), :].astype(jnp.float32)
            total += tile[: ROWS // 2] + tile[ROWS // 2 :]
        inverse[...] = 1.0 / total
        start = start_ref[0]
        lane = lax.broadcasted_iota(jnp.int32, (wide, LANES), 1)
        line = lax.broadcasted_iota(jnp.int32, (wide, LANES), 0)
        pick = jnp.where(lane == start % LANES + line % width, 1.0, 0.0).astype(jnp.bfloat16)
        lane = lax.broadcasted_iota(jnp.int32, (n * ROWS, LANES), 1)
        line = lax.broadcasted_iota(jnp.int32, (n * ROWS, LANES), 0)
        alike = jnp.where(lane % (2 * GROUP) == line % (2 * GROUP), 1.0, 0.0).astype(jnp.bfloat16)
        lane = lax.broadcasted_iota(jnp.int32, (wide, n * ROWS), 1)
        line = lax.broadcasted_iota(jnp.int32, (wide, n * ROWS), 0)
        kept = line // width == lane % (2 * GROUP) // 2
        for g in range(left.shape[0]):
            own = tiles(g, start // LANES)
            raw = lax.dot_general(pick, own, (((1,), (1,)), ((), ())), preferred_element_type=jnp.float32)
            sums = jnp.dot(raw.astype(jnp.bfloat16), alike, preferred_element_type=jnp.float32)
            mean = sums * inverse[:1, :]
            centred = raw - jnp.concatenate([mean] * (n * ROWS // LANES), axis=1)
            centred = jnp.where(kept, centred, 0.0)
            high = centred.astype(jnp.bfloat16)
            left[g, pl.ds(0, wide), :] = high
            left[g, pl.ds(wide, wide), :] = (centred - high.astype(jnp.float32)).astype(jnp.bfloat16)

    for u in range(per_step):
        group = step * per_step + u
        right = jnp.concatenate([tiles(group, q) for q in range(blocks)], axis=1)
        both = jnp.dot(left[group], right, preferred_element_type=jnp.float32)
        product = (both[:wide] + both[wide:]) * inverse[:1, :1]
        out_ref[pl.ds(u * GROUP, GROUP)] = product.reshape(GROUP, width, cycles)


def correlate_call(start, pieces, firsts, before, chunk, cycles, tail):
    n = len(pieces)
    width = cycles // n
    groups = HARMONICS // GROUP // CHUNKS
    steps = groups // 2
    operands = [start, *pieces, *firsts]
    specs = [pl.BlockSpec(memory_space=pltpu.SMEM)] + [pl.BlockSpec(memory_space=pltpu.VMEM)] * (2 * n)
    aliases = {}
    if before is not None:
        aliases = {len(operands): 0}
        operands.append(before)
        specs.append(pl.BlockSpec(memory_space=pl.ANY))
    return pl.pallas_call(
        functools.partial(correlate_kernel, tail),
        out_shape=jax.ShapeDtypeStruct((HARMONICS, width, cycles), jnp.float32),
        grid=(steps,),
        in_specs=specs,
        out_specs=pl.BlockSpec((2 * GROUP, width, cycles), lambda g: (g + chunk * steps, 0, 0)),
        scratch_shapes=[
            pltpu.VMEM((groups, 2 * GROUP * width, n * ROWS), jnp.bfloat16),
            pltpu.VMEM((ROWS // 2, LANES), jnp.float32),
        ],
        input_output_aliases=aliases,
        compiler_params=pltpu.CompilerParams(vmem_limit_bytes=24 << 20),
        cost_estimate=pl.CostEstimate(
            flops=2 * HARMONICS // CHUNKS * width * cycles * n * ROWS,
            bytes_accessed=HARMONICS // CHUNKS * width * cycles * 4,
            transcendentals=0,
        ),
        name="correlate",
    )(*operands)


def chip_at(place, chips):
    place %= chips
    if chips == 8:
        return 2 * place if place < 4 else 2 * (7 - place) + 1
    return place


def gather(piece, n, chunk):
    chips = n // 2
    place = {chip_at(p, chips): p for p in range(chips)}
    ring = {
        sign: [(i, 2 * chip_at(place[i // 2] + sign, chips) + i % 2) for i in range(n)] for sign in (1, -1)
    }
    cores = [(i, i ^ 1) for i in range(n)]
    held = [piece]
    for sign in (1, -1):
        moving = piece
        hops = chips // 2 if (sign == 1) == (chunk % 2 == 0) else chips // 2 - 1
        for _ in range(hops):
            moving = lax.ppermute(moving, "pb", ring[sign])
            held.append(moving)
    return held + [lax.ppermute(x, "pb", cores) for x in held]


def body(frames, valid_mask):
    shots, cycles, angles = frames.shape
    n = lax.axis_size("pb")
    parts = spectra_call(frames, valid_mask)
    start = (lax.axis_index("pb") * (cycles // n)).astype(jnp.int32).reshape(1)
    held = [gather(part, n, chunk) for chunk, part in enumerate(parts)]
    tail = parts[0].shape[0] - ROWS
    out = None
    for chunk in range(CHUNKS):
        out = correlate_call(start, held[chunk], held[0], out, chunk, cycles, tail)
    return out


def solution(mesh):
    placed = (P(("groups", "pb"), None, None), P(("groups", "pb")))
    return jax.shard_map(
        body, mesh=mesh, in_specs=placed, out_specs=P("groups", "pb", None), check_vma=False
    )
```

```python
import math

import jax
import jax.numpy as jnp
import numpy as np
from jax import lax
from jax.experimental import pallas as pl
from jax.experimental.pallas import tpu as pltpu
from jax.sharding import PartitionSpec as P

HARMONICS = 64
LANES = 128
GROUP = 4
ROWS = 4 * GROUP
CHUNKS = 2
PAD = 8
DEPTH = 256


def half_table(angles, first):
    order = 2 * ((np.arange(HARMONICS) + first) % HARMONICS + 1)
    wrapped = np.arange(angles // 2)[:, None] * order[None, :] % angles
    phase = wrapped * (2.0 * math.pi / angles)
    table = np.stack([np.cos(phase), -np.sin(phase)], axis=-1).reshape(angles // 2, 2 * HARMONICS)
    table = (2.0 / math.sqrt(angles)) * table
    high = table.astype(jnp.bfloat16)
    low = (table - high.astype(np.float64)).astype(jnp.bfloat16)
    return np.concatenate([high, low], axis=1)


def spectra_kernel(mask_ref, core_ref, frames_ref, table_ref, *refs):
    out_refs = refs[:CHUNKS]
    buf, table, halves, sems = refs[CHUNKS:]
    shots, cycles, angles = frames_ref.shape
    blocks = cycles // LANES
    half = angles // 2
    groups = HARMONICS // GROUP // CHUNKS
    copies = [pltpu.make_async_copy(table_ref.at[core_ref[0]], table, sems.at[shots * blocks])]
    for q in range(blocks):
        for s in range(shots):
            copies.append(
                pltpu.make_async_copy(
                    frames_ref.at[s, pl.ds(q * LANES, LANES), :], buf.at[q * shots + s], sems.at[q * shots + s]
                )
            )
    for copy in copies:
        copy.start()
    weights = [mask_ref[s].astype(jnp.float32) for s in range(shots)]
    count = jnp.full((PAD, LANES), weights[0] + weights[1], jnp.float32).astype(jnp.bfloat16)
    for out_ref in out_refs:
        out_ref[pl.ds(groups * blocks * ROWS, PAD), :] = count
    copies[0].wait()

    def split(q, s, k):
        scale = 0.5 * weights[s]
        x = buf.at[q * shots + s]
        folded = x[:, pl.ds(k, DEPTH)] * scale + x[:, pl.ds(half + k, DEPTH)] * scale
        high = folded.astype(jnp.bfloat16)
        halves[q % 2, s, pl.ds(0, LANES), pl.ds(k, DEPTH)] = high
        halves[q % 2, s, pl.ds(LANES, LANES), pl.ds(k, DEPTH)] = (folded - high.astype(jnp.float32)).astype(jnp.bfloat16)

    for s in range(shots):
        copies[1 + s].wait()
        for k in range(0, half, DEPTH):
            split(0, s, k)
    for q in range(blocks):
        if q + 1 < blocks:
            for s in range(shots):
                copies[1 + (q + 1) * shots + s].wait()
        pairs = [jnp.zeros((2 * LANES, 2 * LANES), jnp.float32)] * shots
        for k in range(0, half, DEPTH):
            for s in range(shots):
                pairs[s] += jnp.dot(
                    halves[q % 2, s, :, pl.ds(k, DEPTH)], table[pl.ds(k, DEPTH), :], preferred_element_type=jnp.float32
                )
                if q + 1 < blocks:
                    split(q + 1, s, k)
        turned = []
        for pair in pairs:
            pair = pair[:LANES] + pair[LANES:]
            turned.append((pair[:, :LANES] + pair[:, LANES:]).T)
        for g in range(HARMONICS // GROUP):
            part = slice(g * 2 * GROUP, (g + 1) * 2 * GROUP)
            block = jnp.concatenate([turned[0][part], turned[1][part]], axis=0).astype(jnp.bfloat16)
            out_refs[g // groups][pl.ds((g % groups * blocks + q) * ROWS, ROWS), :] = block


def spectra_call(frames, valid_mask, core):
    shots, cycles, angles = frames.shape
    blocks = cycles // LANES
    groups = HARMONICS // GROUP // CHUNKS
    rows = groups * blocks * ROWS + PAD
    table = jnp.asarray(np.stack([half_table(angles, 0), half_table(angles, HARMONICS // CHUNKS)]))
    return pl.pallas_call(
        spectra_kernel,
        out_shape=[jax.ShapeDtypeStruct((rows, LANES), jnp.bfloat16)] * CHUNKS,
        in_specs=[
            pl.BlockSpec(memory_space=pltpu.SMEM),
            pl.BlockSpec(memory_space=pltpu.SMEM),
            pl.BlockSpec(memory_space=pltpu.HBM),
            pl.BlockSpec(memory_space=pltpu.HBM),
        ],
        out_specs=[pl.BlockSpec(memory_space=pltpu.VMEM)] * CHUNKS,
        scratch_shapes=[
            pltpu.VMEM((shots * blocks, LANES, angles), jnp.float32),
            pltpu.VMEM(table.shape[1:], jnp.bfloat16),
            pltpu.VMEM((2, shots, 2 * LANES, angles // 2), jnp.bfloat16),
            pltpu.SemaphoreType.DMA((shots * blocks + 1,)),
        ],
        compiler_params=pltpu.CompilerParams(vmem_limit_bytes=60 << 20),
        cost_estimate=pl.CostEstimate(
            flops=8 * shots * cycles * angles * LANES, bytes_accessed=frames.size * 4, transcendentals=0
        ),
        name="spectra",
    )(valid_mask, core, frames, table)


def correlate_kernel(place_ref, *refs):
    out_ref, left, inverse = refs[-3:]
    n = left.shape[2] // ROWS
    pairs = refs[: n // 2]
    per_step = out_ref.shape[0] // GROUP
    width, cycles = out_ref.shape[1:]
    blocks = cycles // LANES
    wide = GROUP * width
    rows = pairs[0].shape[0] // 2
    step = pl.program_id(0)

    def tiles(group, q):
        at = (group * blocks + q) * ROWS
        return jnp.concatenate(
            [pair[pl.ds(pl.multiple_of(at + half, PAD), ROWS), :] for pair in pairs for half in (0, rows)], axis=0
        )

    @pl.when(step == 0)
    def _():
        total = jnp.zeros((PAD, LANES), jnp.float32)
        for pair in pairs:
            for half in (rows, 2 * rows):
                total += pair[pl.ds(half - PAD, PAD), :].astype(jnp.float32)
        inverse[...] = 1.0 / total
        start = place_ref[0]
        lane = lax.broadcasted_iota(jnp.int32, (wide, LANES), 1)
        line = lax.broadcasted_iota(jnp.int32, (wide, LANES), 0)
        pick = jnp.where(lane == start % LANES + line % width, 1.0, 0.0).astype(jnp.bfloat16)
        lane = lax.broadcasted_iota(jnp.int32, (n * ROWS, LANES), 1)
        line = lax.broadcasted_iota(jnp.int32, (n * ROWS, LANES), 0)
        alike = jnp.where(lane % (2 * GROUP) == line % (2 * GROUP), 1.0, 0.0).astype(jnp.bfloat16)
        lane = lax.broadcasted_iota(jnp.int32, (wide, n * ROWS), 1)
        line = lax.broadcasted_iota(jnp.int32, (wide, n * ROWS), 0)
        kept = line // width == lane % (2 * GROUP) // 2
        for g in range(left.shape[0]):
            own = tiles(g, start // LANES)
            raw = lax.dot_general(pick, own, (((1,), (1,)), ((), ())), preferred_element_type=jnp.float32)
            sums = jnp.dot(raw.astype(jnp.bfloat16), alike, preferred_element_type=jnp.float32)
            mean = sums * inverse[:1, :]
            centred = raw - jnp.concatenate([mean] * (n * ROWS // LANES), axis=1)
            centred = jnp.where(kept, centred, 0.0)
            high = centred.astype(jnp.bfloat16)
            left[g, pl.ds(0, wide), :] = high
            left[g, pl.ds(wide, wide), :] = (centred - high.astype(jnp.float32)).astype(jnp.bfloat16)

    for u in range(per_step):
        group = step * per_step + u
        right = jnp.concatenate([tiles(group, q) for q in range(blocks)], axis=1)
        both = jnp.dot(left[group], right, preferred_element_type=jnp.float32)
        product = (both[:wide] + both[wide:]) * inverse[:1, :1]
        out_ref[pl.ds(u * GROUP, GROUP)] = product.reshape(GROUP, width, cycles)


def correlate_call(place, pairs, before, cycles):
    n = 2 * len(pairs)
    width = cycles // n
    groups = HARMONICS // GROUP // CHUNKS
    steps = groups // 2
    operands = [place, *pairs]
    specs = [pl.BlockSpec(memory_space=pltpu.VMEM)] * len(pairs)
    aliases = {}
    if before is not None:
        aliases = {len(operands): 0}
        operands.append(before)
        specs.append(pl.BlockSpec(memory_space=pl.ANY))
    return pl.pallas_call(
        correlate_kernel,
        out_shape=jax.ShapeDtypeStruct((HARMONICS, width, cycles), jnp.float32),
        grid_spec=pltpu.PrefetchScalarGridSpec(
            num_scalar_prefetch=1,
            grid=(steps,),
            in_specs=specs,
            out_specs=pl.BlockSpec((2 * GROUP, width, cycles), lambda g, at: (g + at[1] * steps, 0, 0)),
            scratch_shapes=[
                pltpu.VMEM((groups, 2 * GROUP * width, n * ROWS), jnp.bfloat16),
                pltpu.VMEM((PAD, LANES), jnp.float32),
            ],
        ),
        input_output_aliases=aliases,
        compiler_params=pltpu.CompilerParams(vmem_limit_bytes=24 << 20),
        cost_estimate=pl.CostEstimate(
            flops=2 * HARMONICS // CHUNKS * width * cycles * n * ROWS,
            bytes_accessed=HARMONICS // CHUNKS * width * cycles * 4,
            transcendentals=0,
        ),
        name="correlate",
    )(*operands)


def chip_at(place, chips):
    place %= chips
    if chips == 8:
        return 2 * place if place < 4 else 2 * (7 - place) + 1
    return place


def move(x, pairs):
    return lax.ppermute(x, "pb", pairs)


def hops(n):
    return n // 4


def gather(mine, n):
    chips = n // 2
    place = {chip_at(p, chips): p for p in range(chips)}
    ring = [(i, 2 * chip_at(place[i // 2] + (-1 if i % 2 else 1), chips) + i % 2) for i in range(n)]
    cores = [(i, i ^ 1) for i in range(n)]
    theirs = [move(mine[1], cores), move(mine[0], cores)]
    first = [jnp.concatenate([mine[0], theirs[0]], axis=0)]
    second = [jnp.concatenate([mine[1], theirs[1]], axis=0)]
    for i in range(1, hops(n) + 1):
        first.append(move(first[-1], ring))
        if i < hops(n):
            second.append(move(second[-1], ring))
    crossed = [[move(x, cores) for x in held[1:]] for held in (first, second)]
    return first + crossed[1], second + crossed[0]


def body(frames, valid_mask):
    _, cycles, _ = frames.shape
    n = lax.axis_size("pb")
    index = lax.axis_index("pb").astype(jnp.int32)
    core = index % 2
    first, second = gather(spectra_call(frames, valid_mask, core.reshape(1)), n)
    start = index * (cycles // n)
    out = correlate_call(jnp.stack([start, core]), first, None, cycles)
    return correlate_call(jnp.stack([start, 1 - core]), second, out, cycles)


def solution(mesh):
    placed = (P(("groups", "pb"), None, None), P(("groups", "pb")))
    return jax.shard_map(body, mesh=mesh, in_specs=placed, out_specs=P("groups", "pb", None), check_vma=False)
```

```python
import functools
import math

import jax
import jax.numpy as jnp
import numpy as np
from jax import lax
from jax.experimental import pallas as pl
from jax.experimental.pallas import tpu as pltpu
from jax.sharding import PartitionSpec as P

HARMONICS = 64
LANES = 128
GROUP = 4
ROWS = 4 * GROUP
CHUNKS = 2
PAD = 8
DEPTH = 256


def half_table(angles, first):
    order = 2 * ((np.arange(HARMONICS) + first) % HARMONICS + 1)
    wrapped = np.arange(angles // 2)[:, None] * order[None, :] % angles
    phase = wrapped * (2.0 * math.pi / angles)
    table = np.stack([np.cos(phase), -np.sin(phase)], axis=-1).reshape(angles // 2, 2 * HARMONICS)
    table = (2.0 / math.sqrt(angles)) * table
    high = table.astype(jnp.bfloat16)
    low = (table - high.astype(np.float64)).astype(jnp.bfloat16)
    return np.concatenate([high, low], axis=1)


def spectra_kernel(mask_ref, frames_ref, table_ref, *refs):
    out_refs = refs[:CHUNKS]
    buf, table, halves, mask, sems = refs[CHUNKS:]
    shots, cycles, angles = frames_ref.shape
    blocks = cycles // LANES
    half = angles // 2
    groups = HARMONICS // GROUP // CHUNKS
    tick = pltpu.make_async_copy(mask_ref, mask, sems.at[shots * blocks + 1])
    tick.start()
    core = lax.rem(lax.axis_index("pb"), 2)
    copies = [pltpu.make_async_copy(table_ref.at[core], table, sems.at[shots * blocks])]
    for q in range(blocks):
        for s in range(shots):
            copies.append(
                pltpu.make_async_copy(
                    frames_ref.at[s, pl.ds(q * LANES, LANES), :], buf.at[q * shots + s], sems.at[q * shots + s]
                )
            )
    for copy in copies:
        copy.start()
    tick.wait()
    weights = [mask[s].astype(jnp.float32) for s in range(shots)]
    count = jnp.full((PAD, LANES), weights[0] + weights[1], jnp.float32).astype(jnp.bfloat16)
    for out_ref in out_refs:
        out_ref[pl.ds(groups * blocks * ROWS, PAD), :] = count
    copies[0].wait()

    def split(q, s, k):
        scale = 0.5 * weights[s]
        x = buf.at[q * shots + s]
        folded = x[:, pl.ds(k, DEPTH)] * scale + x[:, pl.ds(half + k, DEPTH)] * scale
        high = folded.astype(jnp.bfloat16)
        halves[q % 2, s, pl.ds(0, LANES), pl.ds(k, DEPTH)] = high
        halves[q % 2, s, pl.ds(LANES, LANES), pl.ds(k, DEPTH)] = (folded - high.astype(jnp.float32)).astype(jnp.bfloat16)

    for s in range(shots):
        copies[1 + s].wait()
        for k in range(0, half, DEPTH):
            split(0, s, k)
    for q in range(blocks):
        if q + 1 < blocks:
            for s in range(shots):
                copies[1 + (q + 1) * shots + s].wait()
        pairs = [jnp.zeros((2 * LANES, 2 * LANES), jnp.float32)] * shots
        for k in range(0, half, DEPTH):
            for s in range(shots):
                pairs[s] += jnp.dot(
                    halves[q % 2, s, :, pl.ds(k, DEPTH)], table[pl.ds(k, DEPTH), :], preferred_element_type=jnp.float32
                )
                if q + 1 < blocks:
                    split(q + 1, s, k)
        turned = []
        for pair in pairs:
            pair = pair[:LANES] + pair[LANES:]
            turned.append((pair[:, :LANES] + pair[:, LANES:]).T)
        for g in range(HARMONICS // GROUP):
            part = slice(g * 2 * GROUP, (g + 1) * 2 * GROUP)
            block = jnp.concatenate([turned[0][part], turned[1][part]], axis=0).astype(jnp.bfloat16)
            out_refs[g // groups][pl.ds((g % groups * blocks + q) * ROWS, ROWS), :] = block


def spectra_call(frames, valid_mask):
    shots, cycles, angles = frames.shape
    blocks = cycles // LANES
    groups = HARMONICS // GROUP // CHUNKS
    rows = groups * blocks * ROWS + PAD
    table = jnp.asarray(np.stack([half_table(angles, 0), half_table(angles, HARMONICS // CHUNKS)]))
    return pl.pallas_call(
        spectra_kernel,
        out_shape=[jax.ShapeDtypeStruct((rows, LANES), jnp.bfloat16)] * CHUNKS,
        in_specs=[
            pl.BlockSpec(memory_space=pltpu.HBM),
            pl.BlockSpec(memory_space=pltpu.HBM),
            pl.BlockSpec(memory_space=pltpu.HBM),
        ],
        out_specs=[pl.BlockSpec(memory_space=pltpu.VMEM)] * CHUNKS,
        scratch_shapes=[
            pltpu.VMEM((shots * blocks, LANES, angles), jnp.float32),
            pltpu.VMEM(table.shape[1:], jnp.bfloat16),
            pltpu.VMEM((2, shots, 2 * LANES, angles // 2), jnp.bfloat16),
            pltpu.SMEM((shots,), jnp.int32),
            pltpu.SemaphoreType.DMA((shots * blocks + 2,)),
        ],
        compiler_params=pltpu.CompilerParams(vmem_limit_bytes=60 << 20),
        cost_estimate=pl.CostEstimate(
            flops=8 * shots * cycles * angles * LANES, bytes_accessed=frames.size * 4, transcendentals=0
        ),
        name="spectra",
    )(valid_mask, frames, table)


def correlate_kernel(turn, *refs):
    out_ref, left, results, sems = refs[-4:]
    groups, _, n = left.shape
    n //= ROWS
    pairs = refs[: n // 2]
    width, cycles = out_ref.shape[1:]
    blocks = cycles // LANES
    wide = GROUP * width
    rows = pairs[0].shape[0] // 2
    index = lax.axis_index("pb")
    start = index * width
    base = lax.rem(index + turn, 2) * (groups * GROUP)

    def tiles(group, q):
        at = (group * blocks + q) * ROWS
        at = at if isinstance(at, int) else pl.multiple_of(at, PAD)
        return jnp.concatenate([pair[pl.ds(at + half, ROWS), :] for pair in pairs for half in (0, rows)], axis=0)

    total = jnp.zeros((PAD, LANES), jnp.float32)
    for pair in pairs:
        for half in (rows, 2 * rows):
            total += pair[pl.ds(half - PAD, PAD), :].astype(jnp.float32)
    inverse = (1.0 / total)[:1, :]
    lane = lax.broadcasted_iota(jnp.int32, (wide, LANES), 1)
    line = lax.broadcasted_iota(jnp.int32, (wide, LANES), 0)
    pick = jnp.where(lane == lax.rem(start, LANES) + line % width, 1.0, 0.0).astype(jnp.bfloat16)
    lane = lax.broadcasted_iota(jnp.int32, (n * ROWS, LANES), 1)
    line = lax.broadcasted_iota(jnp.int32, (n * ROWS, LANES), 0)
    alike = jnp.where(lane % (2 * GROUP) == line % (2 * GROUP), 1.0, 0.0).astype(jnp.bfloat16)
    lane = lax.broadcasted_iota(jnp.int32, (wide, LANES), 1)
    line = lax.broadcasted_iota(jnp.int32, (wide, LANES), 0)
    kept = line // width == lane % (2 * GROUP) // 2
    kept = jnp.concatenate([kept] * (n * ROWS // LANES), axis=1)

    def prepare(g):
        own = tiles(g, lax.div(start, LANES))
        raw = lax.dot_general(pick, own, (((1,), (1,)), ((), ())), preferred_element_type=jnp.float32)
        sums = jnp.dot(raw.astype(jnp.bfloat16), alike, preferred_element_type=jnp.float32)
        mean = sums * inverse
        centred = raw - jnp.concatenate([mean] * (n * ROWS // LANES), axis=1)
        centred = jnp.where(kept, centred, 0.0)
        high = centred.astype(jnp.bfloat16)
        left[g, pl.ds(0, wide), :] = high
        left[g, pl.ds(wide, wide), :] = (centred - high.astype(jnp.float32)).astype(jnp.bfloat16)

    def copy(g):
        return pltpu.make_async_copy(results.at[g], out_ref.at[pl.ds(base + g * GROUP, GROUP)], sems.at[g])

    prepare(0)
    for g in range(groups):
        if g + 1 < groups:
            prepare(g + 1)
        for q in range(0, blocks, 2):
            right = jnp.concatenate([tiles(g, q), tiles(g, q + 1)], axis=1)
            both = jnp.dot(left[g], right, preferred_element_type=jnp.float32)
            product = (both[:wide] + both[wide:]) * inverse[:, :1]
            results[g, :, :, pl.ds(q * LANES, 2 * LANES)] = product.reshape(GROUP, width, 2 * LANES)
        copy(g).start()
    for g in range(groups):
        copy(g).wait()


def correlate_call(turn, pairs, before, cycles):
    n = 2 * len(pairs)
    width = cycles // n
    groups = HARMONICS // GROUP // CHUNKS
    operands = [*pairs]
    specs = [pl.BlockSpec(memory_space=pltpu.VMEM)] * len(pairs)
    aliases = {}
    if before is not None:
        aliases = {len(operands): 0}
        operands.append(before)
        specs.append(pl.BlockSpec(memory_space=pltpu.HBM))
    return pl.pallas_call(
        functools.partial(correlate_kernel, turn),
        out_shape=jax.ShapeDtypeStruct((HARMONICS, width, cycles), jnp.float32),
        in_specs=specs,
        out_specs=pl.BlockSpec(memory_space=pltpu.HBM),
        scratch_shapes=[
            pltpu.VMEM((groups, 2 * GROUP * width, n * ROWS), jnp.bfloat16),
            pltpu.VMEM((groups, GROUP, width, cycles), jnp.float32),
            pltpu.SemaphoreType.DMA((groups,)),
        ],
        input_output_aliases=aliases,
        compiler_params=pltpu.CompilerParams(vmem_limit_bytes=24 << 20),
        cost_estimate=pl.CostEstimate(
            flops=2 * HARMONICS // CHUNKS * width * cycles * n * ROWS,
            bytes_accessed=HARMONICS // CHUNKS * width * cycles * 4,
            transcendentals=0,
        ),
        name="correlate",
    )(*operands)


def chip_at(place, chips):
    place %= chips
    if chips == 8:
        return 2 * place if place < 4 else 2 * (7 - place) + 1
    return place


def move(x, pairs):
    return lax.ppermute(x, "pb", pairs)


def hops(n):
    return n // 4


def gather(mine, n):
    chips = n // 2
    place = {chip_at(p, chips): p for p in range(chips)}
    ring = [(i, 2 * chip_at(place[i // 2] + (-1 if i % 2 else 1), chips) + i % 2) for i in range(n)]
    cores = [(i, i ^ 1) for i in range(n)]
    theirs = [move(mine[1], cores), move(mine[0], cores)]
    first = [jnp.concatenate([mine[0], theirs[0]], axis=0)]
    second = [jnp.concatenate([mine[1], theirs[1]], axis=0)]
    for i in range(1, hops(n) + 1):
        first.append(move(first[-1], ring))
        if i < hops(n):
            second.append(move(second[-1], ring))
    crossed = [[move(x, cores) for x in held[1:]] for held in (first, second)]
    return first + crossed[1], second + crossed[0]


def body(frames, valid_mask):
    cycles = frames.shape[1]
    first, second = gather(spectra_call(frames, valid_mask), lax.axis_size("pb"))
    out = correlate_call(0, first, None, cycles)
    return correlate_call(1, second, out, cycles)


def solution(mesh):
    placed = (P(("groups", "pb"), None, None), P(("groups", "pb")))
    return jax.shard_map(body, mesh=mesh, in_specs=placed, out_specs=P("groups", "pb", None), check_vma=False)
```
